32 devices in a mesh: tile: 8 (over y, x, core), lat: 4 (over z).
Axes of the slice: x: 2, y: 2, z: 4, core: 2. Of those that a mesh axis runs over, the one named last changes fastest.
Arguments:
- source: bfloat16 [224, 8, 4096], P(('tile', 'lat')), may hold values from -6 to 6
- row_map: bfloat16 [40, 8, 4, 32, 64], P('lat', 'tile'), may hold values from -0.375 to 0.375
- col_map: bfloat16 [40, 4, 64, 2560], P('lat', None, None, 'tile'), may hold values from -0.75 to 0.75
- pattern: int32 [40, 8, 4], P('lat', 'tile'), may hold values from 0 to 11, as said below
- codes: int32 [40, 8, 4], P('lat', 'tile'), may hold values from 0 to 3
- need_list: int32 [8, 4, 12], P('tile'), may hold values from 0 to 223, as said below
- owner: int32 [224], replicated, may hold values from 0 to 223, as said below
Outputs:
- spectrum: float32 [640, 16, 1281], P(('tile', 'lat'))
The draws below stay inside these ranges and needn't reach their ends.
Inputs may be any that keep to these rules, and one draw needn't show every extreme that they name: need_list[t, l] names 12 distinct blocks, all held by devices of tile column t; each device that holds any of them holds exactly 3 of them. `owner`: a permutation of the slots. `pattern`: on each device every one of the 12 indices is used by some term.
All inputs are finite; a program needn't handle non-finite values.
Results may differ from the reference program's by a relative error of at most 0.0029.
Values may be sent and summed in bfloat16 or wider, within the bound.
A program may use at most 64 MiB of HBM per device.

```python
import math
import jax
import jax.numpy as jnp
from jax import lax

NLON = 2560
NLAT = 1280
M = 1280
BS = 64
RB = 32
K = 4
NEED = 12
MOST = 3
SLOTS_DEV = 7
LEV = 8
BLOCKS = 224
N_TILE = 8
N_LAT = 4


def plan_tables(key):
    base = jax.random.fold_in(key, 7301)
    owner = jax.random.permutation(jax.random.fold_in(base, 1), SLOTS_DEV * N_TILE * N_LAT).astype(jnp.int32)
    holders = jnp.argsort(owner, stable=True).astype(jnp.int32)
    groups = NEED // MOST

    def one_device(index):
        device_key = jax.random.fold_in(jax.random.fold_in(base, 2), index)
        column = index // N_LAT
        sources = jax.random.permutation(jax.random.fold_in(device_key, 1), N_LAT)[:groups]

        def one_source(number, holder_lat):
            chosen = jax.random.permutation(jax.random.fold_in(device_key, 10 + number), SLOTS_DEV)[:MOST]
            return (column * N_LAT + holder_lat) * SLOTS_DEV + chosen
        slots = jax.vmap(one_source)(jnp.arange(groups, dtype=jnp.int32), sources).reshape(NEED)
        slots = jax.random.permutation(jax.random.fold_in(device_key, 3), slots)
        return holders[slots]
    needs = jax.vmap(one_device)(jnp.arange(N_TILE * N_LAT, dtype=jnp.int32))
    return (owner, needs.reshape(N_TILE, N_LAT, NEED).astype(jnp.int32))


def draw_owner(key, part):
    return plan_tables(key)[0]


def draw_need_list(key, part):
    return plan_tables(key)[1]


def draw_pattern(key, part):
    base = jax.random.fold_in(key, 5113)
    band = NLAT // (RB * N_LAT)
    total = band * K

    def one_device(index):
        device_key = jax.random.fold_in(base, index)
        head = jax.random.permutation(jax.random.fold_in(device_key, 1), NEED)
        extra = jax.random.randint(jax.random.fold_in(device_key, 2), (total,), 0, NEED)
        values = jnp.concatenate([head, extra[NEED:]])
        values = jax.random.permutation(jax.random.fold_in(device_key, 3), values)
        return values.reshape(band, K)
    table = jax.vmap(one_device)(jnp.arange(N_LAT * N_TILE, dtype=jnp.int32))
    table = table.reshape(N_LAT, N_TILE, band, K)
    return jnp.transpose(table, (0, 2, 1, 3)).reshape(NLAT // RB, N_TILE, K).astype(jnp.int32)


def place_ends(drawn, rng, smallest, largest):
    extent = drawn.shape
    index_at = [jax.random.randint(jax.random.fold_in(rng, axis), (), 0, extent[axis]) for axis in range(len(extent))]
    drawn = drawn.at[tuple(index_at)].set(smallest)
    longest = extent.index(max(extent))
    index_at[longest] = (index_at[longest] + 1) % extent[longest]
    return drawn.at[tuple(index_at)].set(largest)


def levels(rng, extent, shards, smallest, high):
    loudness = 1.0
    for axis_at, shards_of in shards:
        steps = jax.random.uniform(jax.random.fold_in(jax.random.fold_in(rng, 6), axis_at), (shards_of,), jnp.float32, smallest / len(shards), high / len(shards))
        loudness = loudness * jnp.repeat(jnp.exp(steps), extent[axis_at] // shards_of).reshape((-1,) + (1,) * (len(extent) - 1 - axis_at))
    return loudness


def normal_values(rng, shape, spread, most, shards=(), kind=jnp.bfloat16):
    entries = spread * jax.random.normal(rng, shape, jnp.float32)
    if shards:
        entries = entries * levels(rng, shape, shards, -0.22, 0.18)
    return jnp.clip(entries, -most, most).astype(kind)


def setup_inputs(seed: int = 0) -> dict:
    arg_keys = jax.random.split(jax.random.key(seed), 8)
    source = normal_values(arg_keys[0], (BLOCKS, LEV, BS * BS), 1.0, 6.0, ((0, 32),))
    row_map = normal_values(arg_keys[1], (NLAT // RB, N_TILE, K, RB, BS), (K * BS) ** -0.5, 0.375, ((0, 4), (1, 8)))
    col_map = normal_values(arg_keys[2], (NLAT // RB, K, BS, NLON), BS ** -0.5, 0.75, ((0, 4), (3, 8)))
    pattern = draw_pattern(jax.random.fold_in(arg_keys[7], 71), 0)
    codes = place_ends(jax.random.randint(arg_keys[4], (NLAT // RB, N_TILE, K), 0, 4), jax.random.fold_in(arg_keys[4], 1), 0, 3).astype(jnp.int32)
    need_list = draw_need_list(jax.random.fold_in(arg_keys[7], 71), 0)
    owner = draw_owner(jax.random.fold_in(arg_keys[7], 71), 0)
    return dict(source=source, row_map=row_map, col_map=col_map, pattern=pattern, codes=codes, need_list=need_list, owner=owner)


highest = lax.Precision.HIGHEST

def sectoral_logs():
    steps = jnp.arange(1, M, dtype=jnp.int32).astype(jnp.float32)
    terms = 0.5 * jnp.log1p(0.5 / steps)
    return jnp.concatenate([jnp.zeros((1,), jnp.float32), jnp.cumsum(terms)]) + 0.5 * math.log(0.5)

def legendre_sums(fields, pair_ids, colat, weights):
    count = pair_ids.shape[0]
    lats = colat.shape[0]
    norm_logs = sectoral_logs()
    orders = jnp.arange(M, dtype=jnp.int32)
    low_order = pair_ids
    high_order = M - 1 - pair_ids
    low_length = M - pair_ids
    cosine = jnp.cos(colat)
    log_sine = jnp.log(jnp.sin(colat))

    def sectoral(order):
        picked = lax.optimization_barrier(jnp.sum(jnp.where(order[:, None] == orders[None, :], norm_logs[None, :], 0.0), axis=1))
        exponent = picked[:, None] + order.astype(jnp.float32)[:, None] * log_sine[None, :]
        ramp = jnp.clip((exponent + 75.0) / 10.0, 0.0, 1.0)
        return jnp.exp(jnp.maximum(exponent, -75.0)) * ramp
    start_low = sectoral(low_order)
    start_high = sectoral(high_order)
    scaled = fields * weights[None, None, :, None]

    def advance(state, slot):
        previous, before = state
        is_low = slot < low_length
        order = jnp.where(is_low, low_order, high_order)
        degree = jnp.where(is_low, low_order + slot, high_order + slot - low_length)
        fresh = degree == order
        order_f = order.astype(jnp.float32)
        degree_f = degree.astype(jnp.float32)
        lower_f = degree_f - 1.0
        grows = degree > order
        ratio = jnp.where(grows, (4.0 * degree_f * degree_f - 1.0) / jnp.where(grows, degree_f * degree_f - order_f * order_f, 1.0), 0.0)
        back = degree - 1 > order
        inverse = jnp.where(back, (lower_f * lower_f - order_f * order_f) / jnp.where(back, 4.0 * lower_f * lower_f - 1.0, 1.0), 0.0)
        grown = jnp.sqrt(ratio)[:, None] * (cosine[None, :] * previous - jnp.sqrt(inverse)[:, None] * before)
        start = jnp.where(is_low[:, None], start_low, start_high)
        value = jnp.where(fresh[:, None], start, grown)
        return ((value, jnp.where(fresh[:, None], 0.0, previous)), value)

    def one_block(state, base):
        slots = base + jnp.arange(128, dtype=jnp.int32)
        state, table = lax.scan(advance, state, slots, unroll=8)
        low_mask = (slots[:, None] < low_length[None, :]).astype(jnp.float32)
        both = jnp.stack([table * low_mask[:, :, None], table * (1.0 - low_mask)[:, :, None]], axis=2)
        sums = jnp.einsum('sqhl,qhlc->qcs', both, scaled, precision=highest)
        return (state, sums)
    zeros = jnp.zeros((count, lats), jnp.float32)
    total = -(-(M + 1) // 128)
    bases = jnp.arange(total, dtype=jnp.int32) * 128
    _, sums = lax.scan(one_block, (zeros, zeros), bases)
    sums = jnp.transpose(sums, (1, 2, 0, 3)).reshape(count, fields.shape[3], total * 128)
    return sums[:, :, :M + 1]

def row_products(picked, code, rmap, cmap):
    side = rmap.shape[2]
    blocks = picked.reshape(picked.shape[0], picked.shape[1], side, side)
    turned = jnp.swapaxes(blocks, 2, 3)
    chosen = jnp.where((code % 2 == 1)[:, None, None, None], turned, blocks)
    row_flip = (code == 1) | (code == 2)
    col_flip = (code == 2) | (code == 3)
    rmap = jnp.where(row_flip[:, None, None], rmap[:, :, ::-1], rmap)
    cmap = jnp.where(col_flip[:, None, None], cmap[:, ::-1, :], cmap)
    inner = jnp.einsum('klrc,kcx->klrx', chosen.astype(jnp.float32), cmap.astype(jnp.float32), precision=highest)
    inner = lax.optimization_barrier(inner.astype(jnp.bfloat16)).astype(jnp.float32)
    return jnp.einsum('kar,klrx->lax', rmap.astype(jnp.float32), inner, precision=highest)

def reference(source, row_map, col_map, pattern, codes, need_list, owner):
    band = NLAT // (RB * N_LAT)
    width = NLON // N_TILE

    def one_row(row):
        needs = lax.dynamic_index_in_dim(need_list, (row // band).astype(jnp.int32), 1, keepdims=False)
        ids = jnp.take_along_axis(needs, pattern[row], axis=1)
        slots = jnp.take(owner, ids)
        picked = jnp.take(source, slots.reshape(-1), axis=0).reshape((N_TILE, K) + source.shape[1:])
        cmap = jnp.transpose(col_map[row].reshape(K, BS, N_TILE, width), (2, 0, 1, 3))
        rows = jax.vmap(row_products)(picked, codes[row], row_map[row], cmap)
        return jnp.transpose(rows, (1, 2, 0, 3)).reshape(LEV, RB, NLON)
    rows = lax.map(one_row, jnp.arange(NLAT // RB, dtype=jnp.int32))
    field = jnp.transpose(rows, (1, 0, 2, 3)).reshape(LEV, NLAT, NLON)
    spectral = jnp.fft.rfft(field, axis=2)[:, :, :M] / math.sqrt(NLON)
    parts = jnp.stack([jnp.real(spectral), jnp.imag(spectral)]).astype(jnp.float32)
    combined = jnp.transpose(parts, (3, 2, 0, 1)).reshape(M, NLAT, 2 * LEV)
    latitude = jnp.arange(NLAT, dtype=jnp.int32).astype(jnp.float32)
    colat = math.pi * (latitude + 0.75) / (NLAT + 0.5)
    weights = math.pi * jnp.sin(colat) * math.sqrt(NLAT) / (NLAT + 0.5)

    def one_group(group):
        pair_ids = group * 64 + jnp.arange(64, dtype=jnp.int32)
        low = lax.dynamic_slice_in_dim(combined, group * 64, 64, 0)
        high = lax.dynamic_slice_in_dim(combined, M - (group + 1) * 64, 64, 0)[::-1]
        fields = jnp.stack([low, high], axis=1)
        return legendre_sums(fields, pair_ids, colat, weights)
    result = lax.map(one_group, jnp.arange(M // 128, dtype=jnp.int32))
    return result.reshape(M // 2, 2 * LEV, M + 1)
```

```python
import math

import jax
import jax.numpy as jnp
from jax import lax
from jax.experimental import pallas as pl
from jax.experimental.pallas import tpu as pltpu
from jax.sharding import PartitionSpec as P

NLON = 2560
NLAT = 1280
M = 1280
HALF = NLAT // 2
NEED = 12
MOST = 3
LEV = 8
BS = 64
RB = 32
K = 4
QB = 64
SB = 128
SCALE = 1024.0


def permutation(size, flip):
    rows = lax.broadcasted_iota(jnp.int32, (size, size), 0)
    cols = lax.broadcasted_iota(jnp.int32, (size, size), 1)
    target = jnp.where(flip, size - 1 - cols, cols)
    return jnp.where(rows == target, 1.0, 0.0).astype(jnp.bfloat16)


def regrid_kernel(pos, code, south, blocks, rmap, cmap, out, inner, rall):
    g = pl.program_id(0)
    turn = permutation(RB, south[0] == 1)
    for k in range(K):
        c = code[g * K + k]
        where = pos[g * K + k] + NEED * (c % 2)
        picked = blocks[where]
        cols = jnp.dot(permutation(BS, c >= 2), cmap[0, k], preferred_element_type=jnp.float32)
        prod = jnp.dot(picked, cols.astype(jnp.bfloat16), preferred_element_type=jnp.float32)
        inner[:, k * BS : (k + 1) * BS, :] = prod.astype(jnp.bfloat16).reshape(LEV, BS, -1)
        flip = (c == 1) | (c == 2)
        rows = jnp.dot(rmap[0, 0, k], permutation(BS, flip), preferred_element_type=jnp.float32)
        rows = jnp.dot(turn, rows.astype(jnp.bfloat16), preferred_element_type=jnp.float32)
        rall[:, k * BS : (k + 1) * BS] = rows.astype(jnp.bfloat16)
    for lev in range(LEV):
        out[lev] = jnp.dot(rall[...], inner[lev], preferred_element_type=jnp.float32).astype(
            jnp.bfloat16
        )


def regrid(blocks, rmap, cmap, pos, code, south):
    bands = cmap.shape[0]
    width = cmap.shape[3]

    def out_map(g, pos, code, south):
        return (0, jnp.where(south[0] == 1, bands - 1 - g, g), 0)

    return pl.pallas_call(
        regrid_kernel,
        out_shape=jax.ShapeDtypeStruct((LEV, bands * RB, width), jnp.bfloat16),
        grid_spec=pltpu.PrefetchScalarGridSpec(
            num_scalar_prefetch=3,
            grid=(bands,),
            in_specs=[
                pl.BlockSpec(blocks.shape, lambda g, *_: (0, 0, 0)),
                pl.BlockSpec((1, 1, K, RB, BS), lambda g, *_: (g, 0, 0, 0, 0)),
                pl.BlockSpec((1, K, BS, width), lambda g, *_: (g, 0, 0, 0)),
            ],
            out_specs=pl.BlockSpec((LEV, RB, width), out_map),
            scratch_shapes=[
                pltpu.VMEM((LEV, K * BS, width), jnp.bfloat16),
                pltpu.VMEM((RB, K * BS), jnp.bfloat16),
            ],
        ),
        name="regrid",
    )(pos, code, south, blocks, rmap, cmap)


def dft_kernel(rows, base_cos, base_sin, step_cos, step_sin, out, high, low):
    bc = base_cos[...]
    bs = base_sin[...]
    for kind in range(4):
        ca = step_cos[0, kind // 2 : kind // 2 + 1, :]
        sa = step_sin[0, kind // 2 : kind // 2 + 1, :]
        if kind == 0:
            w = ca * bc - sa * bs
        elif kind == 1:
            w = -(sa * bc + ca * bs)
        elif kind == 2:
            w = ca * bc + sa * bs
        else:
            w = ca * bs - sa * bc
        top = w.astype(jnp.bfloat16)
        high[kind * QB : (kind + 1) * QB, :] = top
        low[kind * QB : (kind + 1) * QB, :] = (w - top.astype(jnp.float32)).astype(jnp.bfloat16)
    dims = (((1,), (1,)), ((), ()))
    total = lax.dot_general(high[...], rows[...], dims, preferred_element_type=jnp.float32)
    total += lax.dot_general(low[...], rows[...], dims, preferred_element_type=jnp.float32)
    total = total * (1.0 / math.sqrt(NLON))
    for kind in range(4):
        out[kind] = total[kind * QB : (kind + 1) * QB, :].astype(jnp.bfloat16)


def turns(orders):
    points = jnp.arange(NLON, dtype=jnp.int32)
    phase = orders[..., None] * points % NLON
    angle = phase.astype(jnp.float32) * (2.0 * math.pi / NLON)
    return jnp.cos(angle), jnp.sin(angle)


def dft(rows, tables):
    base_cos, base_sin, step_cos, step_sin = tables
    count = rows.shape[0]
    steps = M // 2 // QB
    return pl.pallas_call(
        dft_kernel,
        out_shape=jax.ShapeDtypeStruct((4, M // 2, count), jnp.bfloat16),
        grid=(steps,),
        in_specs=[
            pl.BlockSpec((count, NLON), lambda j: (0, 0)),
            pl.BlockSpec((QB, NLON), lambda j: (0, 0)),
            pl.BlockSpec((QB, NLON), lambda j: (0, 0)),
            pl.BlockSpec((1, 2, NLON), lambda j: (j, 0, 0)),
            pl.BlockSpec((1, 2, NLON), lambda j: (j, 0, 0)),
        ],
        out_specs=pl.BlockSpec((4, QB, count), lambda j: (0, j, 0)),
        scratch_shapes=[
            pltpu.VMEM((4 * QB, NLON), jnp.bfloat16),
            pltpu.VMEM((4 * QB, NLON), jnp.bfloat16),
        ],
        name="dft",
    )(rows, base_cos, base_sin, step_cos, step_sin)


def dft_tables():
    base = turns(jnp.arange(QB, dtype=jnp.int32))
    first = jnp.arange(M // 2 // QB, dtype=jnp.int32) * QB
    step = turns(jnp.stack([first, M - 1 - first], axis=1))
    return base + step


def legendre_kernel(
    first, fields, x_ref, start_low, start_high, grow, back, out, table, prev_ref, before_ref
):
    pairs = out.shape[0]
    padded = start_low.shape[0]
    first_pair = first[0]
    x = x_ref[...]
    fresh_last = M - first_pair
    fresh_first = fresh_last - padded + 1

    def eight(prev, before, a8, b8, slot, row, careful):
        for k in range(8):
            value = a8[:, k : k + 1] * (x * prev) - b8[:, k : k + 1] * before
            if careful:
                pair = lax.broadcasted_iota(jnp.int32, prev.shape, 0) + first_pair
                value = jnp.where(pair + (slot + k) == M, start_high[...], value)
                value = jnp.where(slot + k == 0, start_low[...], value)
            for lane in range(HALF // 128):
                table[lane, pl.ds(row + k * padded, padded), :] = value[
                    :, lane * 128 : (lane + 1) * 128
                ]
            prev, before = value, prev
        return prev, before

    def block(slot0, count):
        a_block = grow[:, pl.ds(slot0, SB)]
        b_block = back[:, pl.ds(slot0, SB)]

        def some(i, carry):
            prev, before, a8, b8 = carry
            slot = slot0 + i * 8
            row = pl.multiple_of(i * 8 * padded, 8)
            careful = (slot == 0) | ((slot + 7 >= fresh_first) & (slot <= fresh_last))
            prev, before = lax.cond(
                careful,
                lambda p, b: eight(p, b, a8, b8, slot, row, True),
                lambda p, b: eight(p, b, a8, b8, slot, row, False),
                prev,
                before,
            )
            return prev, before, pltpu.roll(a8, SB - 8, 1), pltpu.roll(b8, SB - 8, 1)

        carry = (prev_ref[...], before_ref[...], a_block, b_block)
        prev, before, _, _ = lax.fori_loop(0, count // 8, some, carry)
        prev_ref[...] = prev
        before_ref[...] = before

        @pl.loop(0, pairs)
        def _(q):
            lanes = [
                table[lane, pl.ds(q, count, stride=padded), :] for lane in range(HALF // 128)
            ]
            p32 = jnp.concatenate(lanes, axis=1)
            high = p32.astype(jnp.bfloat16)
            low = (p32 - high.astype(jnp.float32)).astype(jnp.bfloat16)
            dims = (((1,), (1,)), ((), ()))
            field = fields[q]
            sums = lax.dot_general(high, field, dims, preferred_element_type=jnp.float32)
            sums += lax.dot_general(low, field, dims, preferred_element_type=jnp.float32)
            sums = sums.T
            slots = lax.broadcasted_iota(jnp.int32, (2 * LEV, count), 1) + slot0
            length = M - first_pair - q
            is_low = slots < length
            odd = jnp.where(is_low, slots, slots + length) % 2
            sign = jnp.where(odd == 1, -1.0, 1.0)
            c = 2 * LEV
            north = jnp.where(is_low, sums[0:c], sums[2 * c : 3 * c])
            southern = jnp.where(is_low, sums[c : 2 * c], sums[3 * c : 4 * c])
            result = (north + sign * southern) * (1.0 / SCALE)
            if count == SB:
                out[q, :, pl.ds(slot0, SB)] = result
            else:
                out[q, :, M : M + 1] = result[:, 0:1]

    prev_ref[...] = jnp.zeros_like(prev_ref)
    before_ref[...] = jnp.zeros_like(before_ref)

    @pl.loop(0, M // SB)
    def _(b):
        block(pl.multiple_of(b * SB, SB), SB)

    block(M, 8)


def legendre(fields, tables, first):
    x, start_low, start_high, grow, back = tables
    pairs = fields.shape[0]
    padded = start_low.shape[0]
    vmem = pl.BlockSpec(memory_space=pltpu.VMEM)
    return pl.pallas_call(
        legendre_kernel,
        out_shape=jax.ShapeDtypeStruct((pairs, 2 * LEV, M + 1), jnp.float32),
        in_specs=[pl.BlockSpec(memory_space=pltpu.SMEM)] + [vmem] * 6,
        out_specs=vmem,
        scratch_shapes=[
            pltpu.VMEM((HALF // 128, SB * padded, 128), jnp.float32),
            pltpu.VMEM((padded, HALF), jnp.float32),
            pltpu.VMEM((padded, HALF), jnp.float32),
        ],
        name="legendre",
    )(first, fields, x, start_low, start_high, grow, back)


def legendre_tables(first, pairs):
    padded = -(-pairs // 8) * 8
    pair_ids = first + jnp.arange(padded, dtype=jnp.int32)
    latitude = jnp.arange(HALF, dtype=jnp.int32).astype(jnp.float32)
    colat = math.pi * (latitude + 0.75) / (NLAT + 0.5)
    weights = math.pi * jnp.sin(colat) * math.sqrt(NLAT) / (NLAT + 0.5)
    cosine = jnp.cos(colat)
    log_sine = jnp.log(jnp.sin(colat))
    steps = jnp.arange(1, M, dtype=jnp.int32).astype(jnp.float32)
    terms = 0.5 * jnp.log1p(0.5 / steps)
    norm_logs = jnp.concatenate([jnp.zeros((1,), jnp.float32), jnp.cumsum(terms)])
    norm_logs = norm_logs + 0.5 * math.log(0.5)
    orders = jnp.arange(M, dtype=jnp.int32)
    high_order = M - 1 - pair_ids
    low_length = (M - pair_ids)[:, None]

    def sectoral(order):
        picked = jnp.sum(
            jnp.where(order[:, None] == orders[None, :], norm_logs[None, :], 0.0), axis=1
        )
        exponent = picked[:, None] + order.astype(jnp.float32)[:, None] * log_sine[None, :]
        ramp = jnp.clip((exponent + 75.0) / 10.0, 0.0, 1.0)
        value = jnp.exp(jnp.maximum(exponent, -75.0)) * ramp
        return value * (weights * SCALE)[None, :]

    slot = jnp.arange(M + SB, dtype=jnp.int32)[None, :]
    is_low = slot < low_length
    order = jnp.where(is_low, pair_ids[:, None], high_order[:, None])
    degree = order + jnp.where(is_low, slot, slot - low_length)
    order_f = order.astype(jnp.float32)
    degree_f = degree.astype(jnp.float32)
    lower_f = degree_f - 1.0
    grows = degree > order
    ratio = jnp.where(
        grows,
        (4.0 * degree_f * degree_f - 1.0)
        / jnp.where(grows, degree_f * degree_f - order_f * order_f, 1.0),
        0.0,
    )
    behind = degree - 1 > order
    inverse = jnp.where(
        behind,
        (lower_f * lower_f - order_f * order_f)
        / jnp.where(behind, 4.0 * lower_f * lower_f - 1.0, 1.0),
        0.0,
    )
    grow = jnp.sqrt(ratio)
    back = grow * jnp.sqrt(inverse)
    return cosine[None, :], sectoral(pair_ids), sectoral(high_order), grow, back


def body(source, row_map, col_map, pattern, codes, need_list, owner):
    lat_count = lax.axis_size("lat")
    tile_count = lax.axis_size("tile")
    lat_me = lax.axis_index("lat")
    tile_me = lax.axis_index("tile")
    slots_dev = source.shape[0]
    block_ids = jnp.arange(owner.shape[0], dtype=jnp.int32)
    needs_column = need_list[0]
    holder = jnp.sum(
        jnp.where(needs_column[:, :, None] == block_ids[None, None, :], owner[None, None, :], 0),
        axis=2,
    )
    holder_lat = holder // slots_dev % lat_count
    holder_slot = holder % slots_dev
    my_lat = lax.dynamic_index_in_dim(holder_lat, lat_me, 0, keepdims=False)
    held_here = holder_lat == lat_me
    rank = jnp.cumsum(held_here.astype(jnp.int32), axis=1) - 1
    places = jnp.arange(MOST, dtype=jnp.int32)
    hit = held_here[:, None, :] & (rank[:, None, :] == places[None, :, None])
    picks = jnp.sum(jnp.where(hit, holder_slot[:, None, :], 0), axis=2)
    outgoing = jnp.take(source, picks.reshape(-1), axis=0).reshape(
        (lat_count, MOST) + source.shape[1:]
    )
    incoming = lax.all_to_all(outgoing, "lat", split_axis=0, concat_axis=0, tiled=True)
    earlier = jnp.arange(NEED)[:, None] > jnp.arange(NEED)[None, :]
    same = (my_lat[:, None] == my_lat[None, :]) & earlier
    my_rank = jnp.sum(same.astype(jnp.int32), axis=1)
    place = my_lat * MOST + my_rank
    flat = incoming.reshape(lat_count * MOST, LEV, BS, BS)
    return place, flat


def whole(source, row_map, col_map, pattern, codes, need_list, owner):
    lat_count = lax.axis_size("lat")
    tile_count = lax.axis_size("tile")
    lat_me = lax.axis_index("lat")
    tile_me = lax.axis_index("tile")
    place, flat = body(source, row_map, col_map, pattern, codes, need_list, owner)
    held = flat.shape[0]
    uses = pattern[:, 0].reshape(-1)
    wanted = jnp.arange(NEED, dtype=jnp.int32)
    pos = jnp.sum(jnp.where(uses[:, None] == wanted[None, :], place[None, :], 0), axis=1)
    code = codes[:, 0].reshape(-1)
    pos = pos + (held - NEED) * (code % 2)
    blocks = jnp.concatenate([flat, jnp.swapaxes(flat, 2, 3)]).reshape(2 * held, LEV * BS, BS)
    south = (lat_me >= lat_count // 2).astype(jnp.int32).reshape(1)
    field = regrid(blocks, row_map, col_map, pos, code, south)

    flat_rows = field.reshape(LEV * field.shape[1], field.shape[2])
    rows = lax.all_to_all(flat_rows, "tile", split_axis=0, concat_axis=1, tiled=True)
    spectral = dft(rows, dft_tables())
    arranged = lax.all_to_all(spectral, ("tile", "lat"), split_axis=1, concat_axis=0, tiled=True)

    parts = tile_count // LEV
    pairs = M // 2 // (tile_count * lat_count)
    count = rows.shape[0]
    box = arranged.reshape(LEV, parts, lat_count, 2, 2, pairs, count)
    halves = lat_count // 2
    north = box[:, :, :halves]
    southern = box[:, :, halves:][:, :, ::-1]
    both = jnp.stack([north, southern])
    fields = jnp.transpose(both, (6, 4, 0, 5, 1, 3, 2, 7)).reshape(pairs, 8 * LEV, HALF)
    first = (tile_me * lat_count + lat_me) * pairs
    return legendre(fields, legendre_tables(first, pairs), first.reshape(1))


def solution(mesh):
    placed = (
        P(("tile", "lat"), None, None),
        P("lat", "tile", None, None, None),
        P("lat", None, None, "tile"),
        P("lat", "tile", None),
        P("lat", "tile", None),
        P("tile", None, None),
        P(),
    )
    return jax.shard_map(
        whole, mesh=mesh, in_specs=placed, out_specs=P(("tile", "lat"), None, None), check_vma=False
    )
```

```python
import math

import jax
import jax.numpy as jnp
from jax import lax
from jax.experimental import pallas as pl
from jax.experimental.pallas import tpu as pltpu
from jax.sharding import PartitionSpec as P

NLON = 2560
NLAT = 1280
M = 1280
HALF = NLAT // 2
NEED = 12
MOST = 3
LEV = 8
BS = 64
RB = 32
K = 4
QB = 64
SB = 128
AHEAD = 7
SCALE = 1024.0


def permutation(size, flip):
    rows = lax.broadcasted_iota(jnp.int32, (size, size), 0)
    cols = lax.broadcasted_iota(jnp.int32, (size, size), 1)
    target = jnp.where(flip, size - 1 - cols, cols)
    return jnp.where(rows == target, 1.0, 0.0).astype(jnp.bfloat16)


def regrid_kernel(pos, code, south, blocks, rmap, cmap, out, inner, rall):
    g = pl.program_id(0)
    turn = permutation(RB, south[0] == 1)
    for k in range(K):
        c = code[g * K + k]
        where = pos[g * K + k] + NEED * (c % 2)
        picked = blocks[where]
        cols = jnp.dot(permutation(BS, c >= 2), cmap[0, k], preferred_element_type=jnp.float32)
        prod = jnp.dot(picked, cols.astype(jnp.bfloat16), preferred_element_type=jnp.float32)
        inner[:, k * BS : (k + 1) * BS, :] = prod.astype(jnp.bfloat16).reshape(LEV, BS, -1)
        flip = (c == 1) | (c == 2)
        rows = jnp.dot(rmap[0, 0, k], permutation(BS, flip), preferred_element_type=jnp.float32)
        rows = jnp.dot(turn, rows.astype(jnp.bfloat16), preferred_element_type=jnp.float32)
        rall[:, k * BS : (k + 1) * BS] = rows.astype(jnp.bfloat16)
    for lev in range(LEV):
        out[lev] = jnp.dot(rall[...], inner[lev], preferred_element_type=jnp.float32).astype(
            jnp.bfloat16
        )


def regrid(blocks, rmap, cmap, pos, code, south):
    bands = cmap.shape[0]
    width = cmap.shape[3]

    def out_map(g, pos, code, south):
        return (0, jnp.where(south[0] == 1, bands - 1 - g, g), 0)

    return pl.pallas_call(
        regrid_kernel,
        out_shape=jax.ShapeDtypeStruct((LEV, bands * RB, width), jnp.bfloat16),
        grid_spec=pltpu.PrefetchScalarGridSpec(
            num_scalar_prefetch=3,
            grid=(bands,),
            in_specs=[
                pl.BlockSpec(blocks.shape, lambda g, *_: (0, 0, 0)),
                pl.BlockSpec((1, 1, K, RB, BS), lambda g, *_: (g, 0, 0, 0, 0)),
                pl.BlockSpec((1, K, BS, width), lambda g, *_: (g, 0, 0, 0)),
            ],
            out_specs=pl.BlockSpec((LEV, RB, width), out_map),
            scratch_shapes=[
                pltpu.VMEM((LEV, K * BS, width), jnp.bfloat16),
                pltpu.VMEM((RB, K * BS), jnp.bfloat16),
            ],
        ),
        name="regrid",
    )(pos, code, south, blocks, rmap, cmap)


def dft_kernel(rows, base_cos, base_sin, step_cos, step_sin, out, high, low):
    bc = base_cos[...]
    bs = base_sin[...]
    for kind in range(4):
        ca = step_cos[0, kind // 2 : kind // 2 + 1, :]
        sa = step_sin[0, kind // 2 : kind // 2 + 1, :]
        if kind == 0:
            w = ca * bc - sa * bs
        elif kind == 1:
            w = -(sa * bc + ca * bs)
        elif kind == 2:
            w = ca * bc + sa * bs
        else:
            w = ca * bs - sa * bc
        top = w.astype(jnp.bfloat16)
        high[kind * QB : (kind + 1) * QB, :] = top
        low[kind * QB : (kind + 1) * QB, :] = (w - top.astype(jnp.float32)).astype(jnp.bfloat16)
    dims = (((1,), (1,)), ((), ()))
    total = lax.dot_general(high[...], rows[...], dims, preferred_element_type=jnp.float32)
    total += lax.dot_general(low[...], rows[...], dims, preferred_element_type=jnp.float32)
    total = total * (1.0 / math.sqrt(NLON))
    for kind in range(4):
        out[kind] = total[kind * QB : (kind + 1) * QB, :].astype(jnp.bfloat16)


def turns(orders):
    points = jnp.arange(NLON, dtype=jnp.int32)
    phase = orders[..., None] * points % NLON
    angle = phase.astype(jnp.float32) * (2.0 * math.pi / NLON)
    return jnp.cos(angle), jnp.sin(angle)


def dft(rows, tables):
    base_cos, base_sin, step_cos, step_sin = tables
    count = rows.shape[0]
    steps = M // 2 // QB
    return pl.pallas_call(
        dft_kernel,
        out_shape=jax.ShapeDtypeStruct((4, M // 2, count), jnp.bfloat16),
        grid=(steps,),
        in_specs=[
            pl.BlockSpec((count, NLON), lambda j: (0, 0)),
            pl.BlockSpec((QB, NLON), lambda j: (0, 0)),
            pl.BlockSpec((QB, NLON), lambda j: (0, 0)),
            pl.BlockSpec((1, 2, NLON), lambda j: (j, 0, 0)),
            pl.BlockSpec((1, 2, NLON), lambda j: (j, 0, 0)),
        ],
        out_specs=pl.BlockSpec((4, QB, count), lambda j: (0, j, 0)),
        scratch_shapes=[
            pltpu.VMEM((4 * QB, NLON), jnp.bfloat16),
            pltpu.VMEM((4 * QB, NLON), jnp.bfloat16),
        ],
        name="dft",
    )(rows, base_cos, base_sin, step_cos, step_sin)


def dft_tables():
    base = turns(jnp.arange(QB, dtype=jnp.int32))
    first = jnp.arange(M // 2 // QB, dtype=jnp.int32) * QB
    step = turns(jnp.stack([first, M - 1 - first], axis=1))
    return base + step


def recur(first_pair, x, start_low, start_high, grow, back, table, prev_ref, before_ref, slot0, count):
    padded = prev_ref.shape[0]
    fresh_last = M - first_pair
    fresh_first = fresh_last - padded + 1

    def eight(prev, before, a8, b8, slot, row, careful):
        for k in range(8):
            value = a8[:, k : k + 1] * (x * prev) - b8[:, k : k + 1] * before
            if careful:
                pair = lax.broadcasted_iota(jnp.int32, prev.shape, 0) + first_pair
                value = jnp.where(pair + (slot + k) == M, start_high[...], value)
                value = jnp.where(slot + k == 0, start_low[...], value)
            for lane in range(HALF // 128):
                table[lane, pl.ds(row + k * padded, padded), :] = value[
                    :, lane * 128 : (lane + 1) * 128
                ]
            prev, before = value, prev
        return prev, before

    def some(i, carry):
        prev, before, a8, b8 = carry
        slot = slot0 + i * 8
        row = pl.multiple_of(i * 8 * padded, 8)
        careful = (slot == 0) | ((slot + 7 >= fresh_first) & (slot <= fresh_last))
        prev, before = lax.cond(
            careful,
            lambda p, b: eight(p, b, a8, b8, slot, row, True),
            lambda p, b: eight(p, b, a8, b8, slot, row, False),
            prev,
            before,
        )
        return prev, before, pltpu.roll(a8, SB - 8, 1), pltpu.roll(b8, SB - 8, 1)

    a_block = grow[:, pl.ds(slot0, SB)]
    b_block = back[:, pl.ds(slot0, SB)]
    carry = (prev_ref[...], before_ref[...], a_block, b_block)
    prev, before, _, _ = lax.fori_loop(0, count // 8, some, carry)
    prev_ref[...] = prev
    before_ref[...] = before


def split_pair(table, q, count, padded):
    lanes = [table[lane, pl.ds(q, count, stride=padded), :] for lane in range(HALF // 128)]
    exact = jnp.concatenate(lanes, axis=1)
    high = exact.astype(jnp.bfloat16)
    return high, (exact - high.astype(jnp.float32)).astype(jnp.bfloat16)


def unrolled(pairs):
    return 10 if pairs % 10 == 0 else 5 if pairs % 5 == 0 else 1


def ahead_kernel(
    first, x_ref, start_low, start_high, grow, back, out, prev_ref, before_ref, table
):
    pairs = out.shape[1]
    padded = prev_ref.shape[0]
    b = pl.program_id(0)

    @pl.when(b == 0)
    def _():
        prev_ref[...] = jnp.zeros_like(prev_ref)
        before_ref[...] = jnp.zeros_like(before_ref)

    slot0 = pl.multiple_of(b * SB, SB)
    recur(
        first[0], x_ref[...], start_low, start_high, grow, back, table, prev_ref, before_ref,
        slot0, SB,
    )

    @pl.loop(0, pairs, unroll=unrolled(pairs))
    def _(q):
        high, low = split_pair(table, q, SB, padded)
        out[0, q, :, 0:HALF] = high
        out[0, q, :, HALF : 2 * HALF] = low


def ahead(tables, first, pairs):
    x, start_low, start_high, grow, back = tables
    padded = start_low.shape[0]
    full = [pl.BlockSpec(t.shape, lambda b: (0, 0)) for t in tables]
    state = jax.ShapeDtypeStruct((padded, HALF), jnp.float32)
    return pl.pallas_call(
        ahead_kernel,
        out_shape=(
            jax.ShapeDtypeStruct((AHEAD, pairs, SB, 2 * HALF), jnp.bfloat16),
            state,
            state,
        ),
        grid=(AHEAD,),
        in_specs=[pl.BlockSpec(memory_space=pltpu.SMEM)] + full,
        out_specs=(
            pl.BlockSpec((1, pairs, SB, 2 * HALF), lambda b: (b, 0, 0, 0)),
            pl.BlockSpec((padded, HALF), lambda b: (0, 0)),
            pl.BlockSpec((padded, HALF), lambda b: (0, 0)),
        ),
        scratch_shapes=[pltpu.VMEM((HALF // 128, SB * padded, 128), jnp.float32)],
        cost_estimate=pl.CostEstimate(
            flops=40_000_000_000, bytes_accessed=48_000_000, transcendentals=0
        ),
        name="ahead",
    )(first, x, start_low, start_high, grow, back)


def legendre_kernel(
    first, fields, ready, prev_in, before_in, x_ref, start_low, start_high, grow, back, out,
    table, prev_ref, before_ref,
):
    pairs = out.shape[0]
    padded = prev_ref.shape[0]
    first_pair = first[0]
    b = pl.program_id(0)
    slot0 = pl.multiple_of(b * SB, SB)

    def finish(q, high, low, count):
        dims = (((1,), (1,)), ((), ()))
        field = fields[q]
        sums = lax.dot_general(high, field, dims, preferred_element_type=jnp.float32)
        sums += lax.dot_general(low, field, dims, preferred_element_type=jnp.float32)
        sums = sums.T
        slots = lax.broadcasted_iota(jnp.int32, (2 * LEV, count), 1) + slot0
        length = M - first_pair - q
        is_low = slots < length
        odd = jnp.where(is_low, slots, slots + length) % 2
        sign = jnp.where(odd == 1, -1.0, 1.0)
        c = 2 * LEV
        north = jnp.where(is_low, sums[0:c], sums[2 * c : 3 * c])
        southern = jnp.where(is_low, sums[c : 2 * c], sums[3 * c : 4 * c])
        return (north + sign * southern) * (1.0 / SCALE)

    def step(count):
        recur(
            first_pair, x_ref[...], start_low, start_high, grow, back, table, prev_ref,
            before_ref, slot0, count,
        )

    @pl.when(b == 0)
    def _():
        prev_ref[...] = prev_in[...]
        before_ref[...] = before_in[...]

    @pl.when(b < AHEAD)
    def _():
        @pl.loop(0, pairs, unroll=unrolled(pairs))
        def _(q):
            high = ready[0, q, :, 0:HALF]
            low = ready[0, q, :, HALF : 2 * HALF]
            out[q, :, pl.ds(slot0, SB)] = finish(q, high, low, SB)

    @pl.when((b >= AHEAD) & (b < M // SB))
    def _():
        step(SB)

        @pl.loop(0, pairs, unroll=unrolled(pairs))
        def _(q):
            high, low = split_pair(table, q, SB, padded)
            out[q, :, pl.ds(slot0, SB)] = finish(q, high, low, SB)

    @pl.when(b == M // SB)
    def _():
        step(8)

        @pl.loop(0, pairs, unroll=unrolled(pairs))
        def _(q):
            high, low = split_pair(table, q, 8, padded)
            out[q, :, M : M + 1] = finish(q, high, low, 8)[:, 0:1]


def legendre(fields, tables, first, early):
    x, start_low, start_high, grow, back = tables
    ready, prev, before = early
    pairs = fields.shape[0]
    padded = start_low.shape[0]
    full = [pl.BlockSpec(t.shape, lambda b: (0, 0)) for t in (prev, before) + tables]
    return pl.pallas_call(
        legendre_kernel,
        out_shape=jax.ShapeDtypeStruct((pairs, 2 * LEV, M + 1), jnp.float32),
        grid=(M // SB + 1,),
        in_specs=[
            pl.BlockSpec(memory_space=pltpu.SMEM),
            pl.BlockSpec(fields.shape, lambda b: (0, 0, 0)),
            pl.BlockSpec(
                (1, pairs, SB, 2 * HALF), lambda b: (jnp.minimum(b, AHEAD - 1), 0, 0, 0)
            ),
        ]
        + full,
        out_specs=pl.BlockSpec((pairs, 2 * LEV, M + 1), lambda b: (0, 0, 0)),
        scratch_shapes=[
            pltpu.VMEM((HALF // 128, SB * padded, 128), jnp.float32),
            pltpu.VMEM((padded, HALF), jnp.float32),
            pltpu.VMEM((padded, HALF), jnp.float32),
        ],
        name="legendre",
    )(first, fields, ready, prev, before, x, start_low, start_high, grow, back)


def legendre_tables(first, pairs):
    padded = -(-pairs // 8) * 8
    pair_ids = first + jnp.arange(padded, dtype=jnp.int32)
    latitude = jnp.arange(HALF, dtype=jnp.int32).astype(jnp.float32)
    colat = math.pi * (latitude + 0.75) / (NLAT + 0.5)
    weights = math.pi * jnp.sin(colat) * math.sqrt(NLAT) / (NLAT + 0.5)
    cosine = jnp.cos(colat)
    log_sine = jnp.log(jnp.sin(colat))
    steps = jnp.arange(1, M, dtype=jnp.int32).astype(jnp.float32)
    terms = 0.5 * jnp.log1p(0.5 / steps)
    norm_logs = jnp.concatenate([jnp.zeros((1,), jnp.float32), jnp.cumsum(terms)])
    norm_logs = norm_logs + 0.5 * math.log(0.5)
    orders = jnp.arange(M, dtype=jnp.int32)
    high_order = M - 1 - pair_ids
    low_length = (M - pair_ids)[:, None]

    def sectoral(order):
        picked = jnp.sum(
            jnp.where(order[:, None] == orders[None, :], norm_logs[None, :], 0.0), axis=1
        )
        exponent = picked[:, None] + order.astype(jnp.float32)[:, None] * log_sine[None, :]
        ramp = jnp.clip((exponent + 75.0) / 10.0, 0.0, 1.0)
        value = jnp.exp(jnp.maximum(exponent, -75.0)) * ramp
        return value * (weights * SCALE)[None, :]

    slot = jnp.arange(M + SB, dtype=jnp.int32)[None, :]
    is_low = slot < low_length
    order = jnp.where(is_low, pair_ids[:, None], high_order[:, None])
    degree = order + jnp.where(is_low, slot, slot - low_length)
    order_f = order.astype(jnp.float32)
    degree_f = degree.astype(jnp.float32)
    lower_f = degree_f - 1.0
    grows = degree > order
    ratio = jnp.where(
        grows,
        (4.0 * degree_f * degree_f - 1.0)
        / jnp.where(grows, degree_f * degree_f - order_f * order_f, 1.0),
        0.0,
    )
    behind = degree - 1 > order
    inverse = jnp.where(
        behind,
        (lower_f * lower_f - order_f * order_f)
        / jnp.where(behind, 4.0 * lower_f * lower_f - 1.0, 1.0),
        0.0,
    )
    grow = jnp.sqrt(ratio)
    back = grow * jnp.sqrt(inverse)
    return cosine[None, :], sectoral(pair_ids), sectoral(high_order), grow, back


def body(source, row_map, col_map, pattern, codes, need_list, owner):
    lat_count = lax.axis_size("lat")
    tile_count = lax.axis_size("tile")
    lat_me = lax.axis_index("lat")
    tile_me = lax.axis_index("tile")
    slots_dev = source.shape[0]
    block_ids = jnp.arange(owner.shape[0], dtype=jnp.int32)
    needs_column = need_list[0]
    holder = jnp.sum(
        jnp.where(needs_column[:, :, None] == block_ids[None, None, :], owner[None, None, :], 0),
        axis=2,
    )
    holder_lat = holder // slots_dev % lat_count
    holder_slot = holder % slots_dev
    my_lat = lax.dynamic_index_in_dim(holder_lat, lat_me, 0, keepdims=False)
    held_here = holder_lat == lat_me
    rank = jnp.cumsum(held_here.astype(jnp.int32), axis=1) - 1
    places = jnp.arange(MOST, dtype=jnp.int32)
    hit = held_here[:, None, :] & (rank[:, None, :] == places[None, :, None])
    picks = jnp.sum(jnp.where(hit, holder_slot[:, None, :], 0), axis=2)
    outgoing = jnp.take(source, picks.reshape(-1), axis=0).reshape(
        (lat_count, MOST) + source.shape[1:]
    )
    incoming = lax.all_to_all(outgoing, "lat", split_axis=0, concat_axis=0, tiled=True)
    earlier = jnp.arange(NEED)[:, None] > jnp.arange(NEED)[None, :]
    same = (my_lat[:, None] == my_lat[None, :]) & earlier
    my_rank = jnp.sum(same.astype(jnp.int32), axis=1)
    place = my_lat * MOST + my_rank
    flat = incoming.reshape(lat_count * MOST, LEV, BS, BS)
    return place, flat


def whole(source, row_map, col_map, pattern, codes, need_list, owner):
    lat_count = lax.axis_size("lat")
    tile_count = lax.axis_size("tile")
    lat_me = lax.axis_index("lat")
    tile_me = lax.axis_index("tile")
    place, flat = body(source, row_map, col_map, pattern, codes, need_list, owner)
    held = flat.shape[0]
    uses = pattern[:, 0].reshape(-1)
    wanted = jnp.arange(NEED, dtype=jnp.int32)
    pos = jnp.sum(jnp.where(uses[:, None] == wanted[None, :], place[None, :], 0), axis=1)
    code = codes[:, 0].reshape(-1)
    pos = pos + (held - NEED) * (code % 2)
    blocks = jnp.concatenate([flat, jnp.swapaxes(flat, 2, 3)]).reshape(2 * held, LEV * BS, BS)
    south = (lat_me >= lat_count // 2).astype(jnp.int32).reshape(1)
    field = regrid(blocks, row_map, col_map, pos, code, south)

    flat_rows = field.reshape(LEV * field.shape[1], field.shape[2])
    rows = lax.all_to_all(flat_rows, "tile", split_axis=0, concat_axis=1, tiled=True)
    spectral = dft(rows, dft_tables())
    pairs = M // 2 // (tile_count * lat_count)
    first = (tile_me * lat_count + lat_me) * pairs
    tables = legendre_tables(first, pairs)
    spectral, x = lax.optimization_barrier((spectral, tables[0]))
    tables = (x,) + tables[1:]
    early = ahead(tables, first.reshape(1), pairs)
    arranged = lax.all_to_all(spectral, ("tile", "lat"), split_axis=1, concat_axis=0, tiled=True)

    parts = tile_count // LEV
    count = rows.shape[0]
    box = arranged.reshape(LEV, parts, lat_count, 2, 2, pairs, count)
    halves = lat_count // 2
    north = box[:, :, :halves]
    southern = jnp.stack([box[:, :, lat_count - 1 - l] for l in range(halves)], axis=2)
    both = jnp.stack([north, southern])
    fields = jnp.transpose(both, (6, 4, 0, 5, 1, 3, 2, 7)).reshape(pairs, 8 * LEV, HALF)
    return legendre(fields, tables, first.reshape(1), early)


def solution(mesh):
    placed = (
        P(("tile", "lat"), None, None),
        P("lat", "tile", None, None, None),
        P("lat", None, None, "tile"),
        P("lat", "tile", None),
        P("lat", "tile", None),
        P("tile", None, None),
        P(),
    )
    return jax.shard_map(
        whole, mesh=mesh, in_specs=placed, out_specs=P(("tile", "lat"), None, None), check_vma=False
    )
```

```python
import functools
import math

import jax
import jax.numpy as jnp
from jax import lax
from jax.experimental import pallas as pl
from jax.experimental.pallas import tpu as pltpu
from jax.sharding import PartitionSpec as P

NLON = 2560
NLAT = 1280
M = 1280
HALF = NLAT // 2
NEED = 12
MOST = 3
LEV = 8
BS = 64
RB = 32
K = 4
QB = 64
SB = 128
EARLY = 3
LATER = 5
SCALE = 1024.0


def permutation(size, flip):
    rows = lax.broadcasted_iota(jnp.int32, (size, size), 0)
    cols = lax.broadcasted_iota(jnp.int32, (size, size), 1)
    target = jnp.where(flip, size - 1 - cols, cols)
    return jnp.where(rows == target, 1.0, 0.0).astype(jnp.bfloat16)


def regrid_kernel(pos, code, south, blocks, turned, rmap, cmap, out, inner, rall):
    g = pl.program_id(0)
    turn = permutation(RB, south[0] == 1)
    for k in range(K):
        c = code[g * K + k]
        where = pos[g * K + k]
        picked = jnp.where(c % 2 == 1, turned[where], blocks[where])
        cols = jnp.dot(permutation(BS, c >= 2), cmap[0, k], preferred_element_type=jnp.float32)
        prod = jnp.dot(picked, cols.astype(jnp.bfloat16), preferred_element_type=jnp.float32)
        inner[:, k * BS : (k + 1) * BS, :] = prod.astype(jnp.bfloat16).reshape(LEV, BS, -1)
        flip = (c == 1) | (c == 2)
        rows = jnp.dot(rmap[0, 0, k], permutation(BS, flip), preferred_element_type=jnp.float32)
        rows = jnp.dot(turn, rows.astype(jnp.bfloat16), preferred_element_type=jnp.float32)
        rall[:, k * BS : (k + 1) * BS] = rows.astype(jnp.bfloat16)
    for lev in range(LEV):
        out[lev] = jnp.dot(rall[...], inner[lev], preferred_element_type=jnp.float32).astype(
            jnp.bfloat16
        )


def regrid(blocks, turned, rmap, cmap, pos, code, south):
    bands = cmap.shape[0]
    width = cmap.shape[3]

    def out_map(g, pos, code, south):
        return (0, jnp.where(south[0] == 1, bands - 1 - g, g), 0)

    return pl.pallas_call(
        regrid_kernel,
        out_shape=jax.ShapeDtypeStruct((LEV, bands * RB, width), jnp.bfloat16),
        grid_spec=pltpu.PrefetchScalarGridSpec(
            num_scalar_prefetch=3,
            grid=(bands,),
            in_specs=[
                pl.BlockSpec(blocks.shape, lambda g, *_: (0, 0, 0)),
                pl.BlockSpec(blocks.shape, lambda g, *_: (0, 0, 0)),
                pl.BlockSpec((1, 1, K, RB, BS), lambda g, *_: (g, 0, 0, 0, 0)),
                pl.BlockSpec((1, K, BS, width), lambda g, *_: (g, 0, 0, 0)),
            ],
            out_specs=pl.BlockSpec((LEV, RB, width), out_map),
            scratch_shapes=[
                pltpu.VMEM((LEV, K * BS, width), jnp.bfloat16),
                pltpu.VMEM((RB, K * BS), jnp.bfloat16),
            ],
        ),
        name="regrid",
    )(pos, code, south, blocks, turned, rmap, cmap)


def dft_kernel(rows, base_cos, base_sin, step_cos, step_sin, out, high, low):
    bc = base_cos[...]
    bs = base_sin[...]
    for kind in range(4):
        ca = step_cos[0, kind // 2 : kind // 2 + 1, :]
        sa = step_sin[0, kind // 2 : kind // 2 + 1, :]
        if kind == 0:
            w = ca * bc - sa * bs
        elif kind == 1:
            w = -(sa * bc + ca * bs)
        elif kind == 2:
            w = ca * bc + sa * bs
        else:
            w = ca * bs - sa * bc
        top = w.astype(jnp.bfloat16)
        high[kind * QB : (kind + 1) * QB, :] = top
        low[kind * QB : (kind + 1) * QB, :] = (w - top.astype(jnp.float32)).astype(jnp.bfloat16)
    dims = (((1,), (1,)), ((), ()))
    total = lax.dot_general(high[...], rows[...], dims, preferred_element_type=jnp.float32)
    total += lax.dot_general(low[...], rows[...], dims, preferred_element_type=jnp.float32)
    total = total * (1.0 / math.sqrt(NLON))
    for kind in range(4):
        out[kind] = total[kind * QB : (kind + 1) * QB, :].astype(jnp.bfloat16)


def turns(orders):
    points = jnp.arange(NLON, dtype=jnp.int32)
    phase = orders[..., None] * points % NLON
    angle = phase.astype(jnp.float32) * (2.0 * math.pi / NLON)
    return jnp.cos(angle), jnp.sin(angle)


def dft(rows, tables):
    base_cos, base_sin, step_cos, step_sin = tables
    count = rows.shape[0]
    steps = M // 2 // QB
    return pl.pallas_call(
        dft_kernel,
        out_shape=jax.ShapeDtypeStruct((4, M // 2, count), jnp.bfloat16),
        grid=(steps,),
        in_specs=[
            pl.BlockSpec((count, NLON), lambda j: (0, 0)),
            pl.BlockSpec((QB, NLON), lambda j: (0, 0)),
            pl.BlockSpec((QB, NLON), lambda j: (0, 0)),
            pl.BlockSpec((1, 2, NLON), lambda j: (j, 0, 0)),
            pl.BlockSpec((1, 2, NLON), lambda j: (j, 0, 0)),
        ],
        out_specs=pl.BlockSpec((4, QB, count), lambda j: (0, j, 0)),
        scratch_shapes=[
            pltpu.VMEM((4 * QB, NLON), jnp.bfloat16),
            pltpu.VMEM((4 * QB, NLON), jnp.bfloat16),
        ],
        name="dft",
    )(rows, base_cos, base_sin, step_cos, step_sin)


def dft_tables():
    base = turns(jnp.arange(QB, dtype=jnp.int32))
    first = jnp.arange(M // 2 // QB, dtype=jnp.int32) * QB
    step = turns(jnp.stack([first, M - 1 - first], axis=1))
    return base + step


def recur(first_pair, x, start_low, start_high, grow, back, table, prev_ref, before_ref, slot0, count):
    padded = prev_ref.shape[0]
    fresh_last = M - first_pair
    fresh_first = fresh_last - padded + 1

    def eight(prev, before, a8, b8, slot, row, careful):
        for k in range(8):
            value = a8[:, k : k + 1] * (x * prev) - b8[:, k : k + 1] * before
            if careful:
                pair = lax.broadcasted_iota(jnp.int32, prev.shape, 0) + first_pair
                value = jnp.where(pair + (slot + k) == M, start_high[...], value)
                value = jnp.where(slot + k == 0, start_low[...], value)
            for lane in range(HALF // 128):
                table[lane, pl.ds(row + k * padded, padded), :] = value[
                    :, lane * 128 : (lane + 1) * 128
                ]
            prev, before = value, prev
        return prev, before

    def some(i, carry):
        prev, before, a8, b8 = carry
        slot = slot0 + i * 8
        row = pl.multiple_of(i * 8 * padded, 8)
        careful = (slot == 0) | ((slot + 7 >= fresh_first) & (slot <= fresh_last))
        prev, before = lax.cond(
            careful,
            lambda p, b: eight(p, b, a8, b8, slot, row, True),
            lambda p, b: eight(p, b, a8, b8, slot, row, False),
            prev,
            before,
        )
        return prev, before, pltpu.roll(a8, SB - 8, 1), pltpu.roll(b8, SB - 8, 1)

    a_block = grow[:, pl.ds(slot0, SB)]
    b_block = back[:, pl.ds(slot0, SB)]
    carry = (prev_ref[...], before_ref[...], a_block, b_block)
    prev, before, _, _ = lax.fori_loop(0, count // 8, some, carry)
    prev_ref[...] = prev
    before_ref[...] = before


def split_pair(table, q, count, padded):
    lanes = [table[lane, pl.ds(q, count, stride=padded), :] for lane in range(HALF // 128)]
    exact = jnp.concatenate(lanes, axis=1)
    high = exact.astype(jnp.bfloat16)
    return high, (exact - high.astype(jnp.float32)).astype(jnp.bfloat16)


def unrolled(pairs):
    return 10 if pairs % 10 == 0 else 5 if pairs % 5 == 0 else 1


def ahead_kernel(
    begin, first, prev_in, before_in, x_ref, start_low, start_high, grow, back, out, prev_ref, before_ref, table
):
    pairs = out.shape[1]
    padded = prev_ref.shape[0]
    b = pl.program_id(0)

    @pl.when(b == 0)
    def _():
        prev_ref[...] = prev_in[...]
        before_ref[...] = before_in[...]

    slot0 = pl.multiple_of((b + begin) * SB, SB)
    recur(
        first[0], x_ref[...], start_low, start_high, grow, back, table, prev_ref, before_ref,
        slot0, SB,
    )

    @pl.loop(0, pairs, unroll=unrolled(pairs))
    def _(q):
        high, low = split_pair(table, q, SB, padded)
        out[0, q, :, 0:HALF] = high
        out[0, q, :, HALF : 2 * HALF] = low


def ahead(tables, first, pairs, begin, blocks, prev, before):
    x, start_low, start_high, grow, back = tables
    padded = start_low.shape[0]
    full = [pl.BlockSpec(t.shape, lambda b: (0, 0)) for t in (prev, before) + tables]
    state = jax.ShapeDtypeStruct((padded, HALF), jnp.float32)
    return pl.pallas_call(
        functools.partial(ahead_kernel, begin),
        out_shape=(
            jax.ShapeDtypeStruct((blocks, pairs, SB, 2 * HALF), jnp.bfloat16),
            state,
            state,
        ),
        grid=(blocks,),
        in_specs=[pl.BlockSpec(memory_space=pltpu.SMEM)] + full,
        out_specs=(
            pl.BlockSpec((1, pairs, SB, 2 * HALF), lambda b: (b, 0, 0, 0)),
            pl.BlockSpec((padded, HALF), lambda b: (0, 0)),
            pl.BlockSpec((padded, HALF), lambda b: (0, 0)),
        ),
        scratch_shapes=[pltpu.VMEM((HALF // 128, SB * padded, 128), jnp.float32)],
        cost_estimate=pl.CostEstimate(
            flops=blocks * 6_000_000_000, bytes_accessed=blocks * 7_000_000, transcendentals=0
        ),
        name=f"ahead{begin}",
    )(first, prev, before, x, start_low, start_high, grow, back)


def legendre_kernel(
    width, first, raw, ready, later, prev_in, before_in, x_ref, start_low, start_high, grow, back, out,
    fields, table, prev_ref, before_ref,
):
    pairs = out.shape[0]
    padded = prev_ref.shape[0]
    first_pair = first[0]
    b = pl.program_id(0)
    slot0 = pl.multiple_of(b * SB, SB)

    def finish(q, high, low, count):
        dims = (((1,), (1,)), ((), ()))
        field = fields[q]
        sums = lax.dot_general(high, field, dims, preferred_element_type=jnp.float32)
        sums += lax.dot_general(low, field, dims, preferred_element_type=jnp.float32)
        sums = sums.T
        slots = lax.broadcasted_iota(jnp.int32, (2 * LEV, count), 1) + slot0
        length = M - first_pair - q
        is_low = slots < length
        odd = jnp.where(is_low, slots, slots + length) % 2
        sign = jnp.where(odd == 1, -1.0, 1.0)
        c = 2 * LEV
        north = jnp.where(is_low, sums[0:c], sums[2 * c : 3 * c])
        southern = jnp.where(is_low, sums[c : 2 * c], sums[3 * c : 4 * c])
        return (north + sign * southern) * (1.0 / SCALE)

    def step(count):
        recur(
            first_pair, x_ref[...], start_low, start_high, grow, back, table, prev_ref,
            before_ref, slot0, count,
        )

    @pl.when(b == 0)
    def _():
        prev_ref[...] = prev_in[...]
        before_ref[...] = before_in[...]

        @pl.loop(0, pairs)
        def _(q):
            c = 2 * LEV
            for upper in range(2):
                part = raw[q, upper * c : (upper + 1) * c, :]
                bands = [
                    part[:, at : at + width] for at in range(NLAT - width, HALF - 1, -width)
                ]
                fields[q, 2 * upper * c : (2 * upper + 1) * c, :] = part[:, 0:HALF]
                fields[q, (2 * upper + 1) * c : (2 * upper + 2) * c, :] = jnp.concatenate(
                    bands, axis=1
                )

    def from_store(store):
        @pl.loop(0, pairs, unroll=unrolled(pairs))
        def _(q):
            high = store[0, q, :, 0:HALF]
            low = store[0, q, :, HALF : 2 * HALF]
            out[q, :, pl.ds(slot0, SB)] = finish(q, high, low, SB)

    @pl.when(b < EARLY)
    def _():
        from_store(ready)

    @pl.when((b >= EARLY) & (b < EARLY + LATER))
    def _():
        from_store(later)

    @pl.when((b >= EARLY + LATER) & (b < M // SB))
    def _():
        step(SB)

        @pl.loop(0, pairs, unroll=unrolled(pairs))
        def _(q):
            high, low = split_pair(table, q, SB, padded)
            out[q, :, pl.ds(slot0, SB)] = finish(q, high, low, SB)

    @pl.when(b == M // SB)
    def _():
        step(8)

        @pl.loop(0, pairs, unroll=unrolled(pairs))
        def _(q):
            high, low = split_pair(table, q, 8, padded)
            out[q, :, M : M + 1] = finish(q, high, low, 8)[:, 0:1]


def legendre(raw, tables, first, ready, late, width):
    x, start_low, start_high, grow, back = tables
    later, prev, before = late
    pairs = raw.shape[0]
    padded = start_low.shape[0]
    full = [pl.BlockSpec(t.shape, lambda b: (0, 0)) for t in (prev, before) + tables]
    return pl.pallas_call(
        functools.partial(legendre_kernel, width),
        out_shape=jax.ShapeDtypeStruct((pairs, 2 * LEV, M + 1), jnp.float32),
        grid=(M // SB + 1,),
        in_specs=[
            pl.BlockSpec(memory_space=pltpu.SMEM),
            pl.BlockSpec(raw.shape, lambda b: (0, 0, 0)),
            pl.BlockSpec(
                (1, pairs, SB, 2 * HALF), lambda b: (jnp.minimum(b, EARLY - 1), 0, 0, 0)
            ),
            pl.BlockSpec(
                (1, pairs, SB, 2 * HALF),
                lambda b: (jnp.clip(b - EARLY, 0, LATER - 1), 0, 0, 0),
            ),
        ]
        + full,
        out_specs=pl.BlockSpec((pairs, 2 * LEV, M + 1), lambda b: (0, 0, 0)),
        scratch_shapes=[
            pltpu.VMEM((pairs, 8 * LEV, HALF), jnp.bfloat16),
            pltpu.VMEM((HALF // 128, SB * padded, 128), jnp.float32),
            pltpu.VMEM((padded, HALF), jnp.float32),
            pltpu.VMEM((padded, HALF), jnp.float32),
        ],
        name="legendre",
    )(first, raw, ready, later, prev, before, x, start_low, start_high, grow, back)


def legendre_tables(first, pairs):
    padded = -(-pairs // 8) * 8
    pair_ids = first + jnp.arange(padded, dtype=jnp.int32)
    latitude = jnp.arange(HALF, dtype=jnp.int32).astype(jnp.float32)
    colat = math.pi * (latitude + 0.75) / (NLAT + 0.5)
    weights = math.pi * jnp.sin(colat) * math.sqrt(NLAT) / (NLAT + 0.5)
    cosine = jnp.cos(colat)
    log_sine = jnp.log(jnp.sin(colat))
    steps = jnp.arange(1, M, dtype=jnp.int32).astype(jnp.float32)
    terms = 0.5 * jnp.log1p(0.5 / steps)
    norm_logs = jnp.concatenate([jnp.zeros((1,), jnp.float32), jnp.cumsum(terms)])
    norm_logs = norm_logs + 0.5 * math.log(0.5)
    orders = jnp.arange(M, dtype=jnp.int32)
    high_order = M - 1 - pair_ids
    low_length = (M - pair_ids)[:, None]

    def sectoral(order):
        picked = jnp.sum(
            jnp.where(order[:, None] == orders[None, :], norm_logs[None, :], 0.0), axis=1
        )
        exponent = picked[:, None] + order.astype(jnp.float32)[:, None] * log_sine[None, :]
        ramp = jnp.clip((exponent + 75.0) / 10.0, 0.0, 1.0)
        value = jnp.exp(jnp.maximum(exponent, -75.0)) * ramp
        return value * (weights * SCALE)[None, :]

    slot = jnp.arange(M + SB, dtype=jnp.int32)[None, :]
    is_low = slot < low_length
    order = jnp.where(is_low, pair_ids[:, None], high_order[:, None])
    degree = order + jnp.where(is_low, slot, slot - low_length)
    order_f = order.astype(jnp.float32)
    degree_f = degree.astype(jnp.float32)
    lower_f = degree_f - 1.0
    grows = degree > order
    ratio = jnp.where(
        grows,
        (4.0 * degree_f * degree_f - 1.0)
        / jnp.where(grows, degree_f * degree_f - order_f * order_f, 1.0),
        0.0,
    )
    behind = degree - 1 > order
    inverse = jnp.where(
        behind,
        (lower_f * lower_f - order_f * order_f)
        / jnp.where(behind, 4.0 * lower_f * lower_f - 1.0, 1.0),
        0.0,
    )
    grow = jnp.sqrt(ratio)
    back = grow * jnp.sqrt(inverse)
    return cosine[None, :], sectoral(pair_ids), sectoral(high_order), grow, back


def body(source, row_map, col_map, pattern, codes, need_list, owner):
    lat_count = lax.axis_size("lat")
    tile_count = lax.axis_size("tile")
    lat_me = lax.axis_index("lat")
    tile_me = lax.axis_index("tile")
    slots_dev = source.shape[0]
    block_ids = jnp.arange(owner.shape[0], dtype=jnp.int32)
    needs_column = need_list[0]
    holder = jnp.sum(
        jnp.where(needs_column[:, :, None] == block_ids[None, None, :], owner[None, None, :], 0),
        axis=2,
    )
    holder_lat = holder // slots_dev % lat_count
    holder_slot = holder % slots_dev
    my_lat = lax.dynamic_index_in_dim(holder_lat, lat_me, 0, keepdims=False)
    held_here = holder_lat == lat_me
    rank = jnp.cumsum(held_here.astype(jnp.int32), axis=1) - 1
    places = jnp.arange(MOST, dtype=jnp.int32)
    hit = held_here[:, None, :] & (rank[:, None, :] == places[None, :, None])
    picks = jnp.sum(jnp.where(hit, holder_slot[:, None, :], 0), axis=2)
    outgoing = jnp.take(source, picks.reshape(-1), axis=0).reshape(
        (lat_count, MOST) + source.shape[1:]
    )
    incoming = lax.all_to_all(outgoing, "lat", split_axis=0, concat_axis=0, tiled=True)
    earlier = jnp.arange(NEED)[:, None] > jnp.arange(NEED)[None, :]
    same = (my_lat[:, None] == my_lat[None, :]) & earlier
    my_rank = jnp.sum(same.astype(jnp.int32), axis=1)
    place = my_lat * MOST + my_rank
    flat = incoming.reshape(lat_count * MOST, LEV, BS, BS)
    return place, flat


def whole(source, row_map, col_map, pattern, codes, need_list, owner):
    lat_count = lax.axis_size("lat")
    tile_count = lax.axis_size("tile")
    lat_me = lax.axis_index("lat")
    tile_me = lax.axis_index("tile")
    place, flat = body(source, row_map, col_map, pattern, codes, need_list, owner)
    held = flat.shape[0]
    uses = pattern[:, 0].reshape(-1)
    wanted = jnp.arange(NEED, dtype=jnp.int32)
    pos = jnp.sum(jnp.where(uses[:, None] == wanted[None, :], place[None, :], 0), axis=1)
    code = codes[:, 0].reshape(-1)
    blocks = flat.reshape(held, LEV * BS, BS)
    turned = jnp.swapaxes(flat, 2, 3).reshape(held, LEV * BS, BS)
    south = (lat_me >= lat_count // 2).astype(jnp.int32).reshape(1)
    field = regrid(blocks, turned, row_map, col_map, pos, code, south)

    pairs = M // 2 // (tile_count * lat_count)
    first = (tile_me * lat_count + lat_me) * pairs
    tables = legendre_tables(first, pairs)
    field, x = lax.optimization_barrier((field, tables[0]))
    tables = (x,) + tables[1:]
    zeros = jnp.zeros_like(tables[1])
    ready, prev, before = ahead(tables, first.reshape(1), pairs, 0, EARLY, zeros, zeros)

    flat_rows = field.reshape(LEV * field.shape[1], field.shape[2])
    rows = lax.all_to_all(flat_rows, "tile", split_axis=0, concat_axis=1, tiled=True)
    spectral = dft(rows, dft_tables())
    spectral, prev = lax.optimization_barrier((spectral, prev))
    late = ahead(tables, first.reshape(1), pairs, EARLY, LATER, prev, before)
    arranged = lax.all_to_all(spectral, ("tile", "lat"), split_axis=1, concat_axis=0, tiled=True)

    parts = tile_count // LEV
    count = rows.shape[0]
    box = arranged.reshape(LEV, parts, lat_count, 2, 2, pairs, count)
    raw = jnp.transpose(box, (5, 3, 4, 0, 2, 1, 6)).reshape(pairs, 4 * LEV, NLAT)
    return legendre(raw, tables, first.reshape(1), ready, late, NLAT // lat_count)


def solution(mesh):
    placed = (
        P(("tile", "lat"), None, None),
        P("lat", "tile", None, None, None),
        P("lat", None, None, "tile"),
        P("lat", "tile", None),
        P("lat", "tile", None),
        P("tile", None, None),
        P(),
    )
    return jax.shard_map(
        whole, mesh=mesh, in_specs=placed, out_specs=P(("tile", "lat"), None, None), check_vma=False
    )
```

```python
import functools
import math

import jax
import jax.numpy as jnp
from jax import lax
from jax.experimental import pallas as pl
from jax.experimental.pallas import tpu as pltpu
from jax.sharding import PartitionSpec as P

NLON = 2560
NLAT = 1280
M = 1280
HALF = NLAT // 2
NEED = 12
MOST = 3
LEV = 8
BS = 64
RB = 32
K = 4
QB = 64
SB = 128
EARLY = 3
LATER = 5
SCALE = 1024.0


def permutation(size, flip):
    rows = lax.broadcasted_iota(jnp.int32, (size, size), 0)
    cols = lax.broadcasted_iota(jnp.int32, (size, size), 1)
    target = jnp.where(flip, size - 1 - cols, cols)
    return jnp.where(rows == target, 1.0, 0.0).astype(jnp.bfloat16)


def regrid_kernel(pos, code, south, blocks, turned, rmap, cmap, out, inner, rall):
    g = pl.program_id(0)
    turn = permutation(RB, south[0] == 1)
    for k in range(K):
        c = code[g * K + k]
        where = pos[g * K + k]
        picked = jnp.where(c % 2 == 1, turned[where], blocks[where])
        cols = jnp.dot(permutation(BS, c >= 2), cmap[0, k], preferred_element_type=jnp.float32)
        prod = jnp.dot(picked, cols.astype(jnp.bfloat16), preferred_element_type=jnp.float32)
        inner[:, k * BS : (k + 1) * BS, :] = prod.astype(jnp.bfloat16).reshape(LEV, BS, -1)
        flip = (c == 1) | (c == 2)
        rows = jnp.dot(rmap[0, 0, k], permutation(BS, flip), preferred_element_type=jnp.float32)
        rows = jnp.dot(turn, rows.astype(jnp.bfloat16), preferred_element_type=jnp.float32)
        rall[:, k * BS : (k + 1) * BS] = rows.astype(jnp.bfloat16)
    for lev in range(LEV):
        out[lev] = jnp.dot(rall[...], inner[lev], preferred_element_type=jnp.float32).astype(
            jnp.bfloat16
        )


def regrid(blocks, turned, rmap, cmap, pos, code, south):
    bands = cmap.shape[0]
    width = cmap.shape[3]

    def out_map(g, pos, code, south):
        return (0, jnp.where(south[0] == 1, bands - 1 - g, g), 0)

    return pl.pallas_call(
        regrid_kernel,
        out_shape=jax.ShapeDtypeStruct((LEV, bands * RB, width), jnp.bfloat16),
        grid_spec=pltpu.PrefetchScalarGridSpec(
            num_scalar_prefetch=3,
            grid=(bands,),
            in_specs=[
                pl.BlockSpec(blocks.shape, lambda g, *_: (0, 0, 0)),
                pl.BlockSpec(blocks.shape, lambda g, *_: (0, 0, 0)),
                pl.BlockSpec((1, 1, K, RB, BS), lambda g, *_: (g, 0, 0, 0, 0)),
                pl.BlockSpec((1, K, BS, width), lambda g, *_: (g, 0, 0, 0)),
            ],
            out_specs=pl.BlockSpec((LEV, RB, width), out_map),
            scratch_shapes=[
                pltpu.VMEM((LEV, K * BS, width), jnp.bfloat16),
                pltpu.VMEM((RB, K * BS), jnp.bfloat16),
            ],
        ),
        name="regrid",
    )(pos, code, south, blocks, turned, rmap, cmap)


def dft_kernel(rows, base_cos, base_sin, step_cos, step_sin, out, high, low):
    bc = base_cos[...]
    bs = base_sin[...]
    for kind in range(4):
        ca = step_cos[0, kind // 2 : kind // 2 + 1, :]
        sa = step_sin[0, kind // 2 : kind // 2 + 1, :]
        if kind == 0:
            w = ca * bc - sa * bs
        elif kind == 1:
            w = -(sa * bc + ca * bs)
        elif kind == 2:
            w = ca * bc + sa * bs
        else:
            w = ca * bs - sa * bc
        top = w.astype(jnp.bfloat16)
        high[kind * QB : (kind + 1) * QB, :] = top
        low[kind * QB : (kind + 1) * QB, :] = (w - top.astype(jnp.float32)).astype(jnp.bfloat16)
    dims = (((1,), (1,)), ((), ()))
    total = lax.dot_general(high[...], rows[...], dims, preferred_element_type=jnp.float32)
    total += lax.dot_general(low[...], rows[...], dims, preferred_element_type=jnp.float32)
    total = total * (1.0 / math.sqrt(NLON))
    for kind in range(4):
        out[kind] = total[kind * QB : (kind + 1) * QB, :].astype(jnp.bfloat16)


def turns(orders):
    points = jnp.arange(NLON, dtype=jnp.int32)
    phase = orders[..., None] * points % NLON
    angle = phase.astype(jnp.float32) * (2.0 * math.pi / NLON)
    return jnp.cos(angle), jnp.sin(angle)


def dft(rows, tables):
    base_cos, base_sin, step_cos, step_sin = tables
    count = rows.shape[0]
    steps = M // 2 // QB
    return pl.pallas_call(
        dft_kernel,
        out_shape=jax.ShapeDtypeStruct((4, M // 2, count), jnp.bfloat16),
        grid=(steps,),
        in_specs=[
            pl.BlockSpec((count, NLON), lambda j: (0, 0)),
            pl.BlockSpec((QB, NLON), lambda j: (0, 0)),
            pl.BlockSpec((QB, NLON), lambda j: (0, 0)),
            pl.BlockSpec((1, 2, NLON), lambda j: (j, 0, 0)),
            pl.BlockSpec((1, 2, NLON), lambda j: (j, 0, 0)),
        ],
        out_specs=pl.BlockSpec((4, QB, count), lambda j: (0, j, 0)),
        scratch_shapes=[
            pltpu.VMEM((4 * QB, NLON), jnp.bfloat16),
            pltpu.VMEM((4 * QB, NLON), jnp.bfloat16),
        ],
        name="dft",
    )(rows, base_cos, base_sin, step_cos, step_sin)


def dft_tables():
    base = turns(jnp.arange(QB, dtype=jnp.int32))
    first = jnp.arange(M // 2 // QB, dtype=jnp.int32) * QB
    step = turns(jnp.stack([first, M - 1 - first], axis=1))
    return base + step


def recur(first_pair, x, start_low, start_high, grow, back, table, prev_ref, before_ref, slot0, count):
    padded = prev_ref.shape[0]
    fresh_last = M - first_pair
    fresh_first = fresh_last - padded + 1

    def eight(prev, before, a8, b8, slot, row, careful):
        for k in range(8):
            value = a8[:, k : k + 1] * (x * prev) - b8[:, k : k + 1] * before
            if careful:
                pair = lax.broadcasted_iota(jnp.int32, prev.shape, 0) + first_pair
                value = jnp.where(pair + (slot + k) == M, start_high[...], value)
                value = jnp.where(slot + k == 0, start_low[...], value)
            for lane in range(HALF // 128):
                table[lane, pl.ds(row + k * padded, padded), :] = value[
                    :, lane * 128 : (lane + 1) * 128
                ]
            prev, before = value, prev
        return prev, before

    def some(i, carry):
        prev, before, a8, b8 = carry
        slot = slot0 + i * 8
        row = pl.multiple_of(i * 8 * padded, 8)
        careful = (slot == 0) | ((slot + 7 >= fresh_first) & (slot <= fresh_last))
        prev, before = lax.cond(
            careful,
            lambda p, b: eight(p, b, a8, b8, slot, row, True),
            lambda p, b: eight(p, b, a8, b8, slot, row, False),
            prev,
            before,
        )
        return prev, before, pltpu.roll(a8, SB - 8, 1), pltpu.roll(b8, SB - 8, 1)

    a_block = grow[:, pl.ds(slot0, SB)]
    b_block = back[:, pl.ds(slot0, SB)]
    carry = (prev_ref[...], before_ref[...], a_block, b_block)
    prev, before, _, _ = lax.fori_loop(0, count // 8, some, carry)
    prev_ref[...] = prev
    before_ref[...] = before


def split_pair(table, q, count, padded):
    lanes = [table[lane, pl.ds(q, count, stride=padded), :] for lane in range(HALF // 128)]
    exact = jnp.concatenate(lanes, axis=1)
    high = exact.astype(jnp.bfloat16)
    return high, (exact - high.astype(jnp.float32)).astype(jnp.bfloat16)


def unrolled(pairs):
    return 20 if pairs % 20 == 0 else 5 if pairs % 5 == 0 else 1


def ahead_kernel(
    begin, first, prev_in, before_in, x_ref, start_low, start_high, grow, back, out, prev_ref, before_ref, table
):
    pairs = out.shape[1]
    padded = prev_ref.shape[0]
    b = pl.program_id(0)

    @pl.when(b == 0)
    def _():
        prev_ref[...] = prev_in[...]
        before_ref[...] = before_in[...]

    slot0 = pl.multiple_of((b + begin) * SB, SB)
    recur(
        first[0], x_ref[...], start_low, start_high, grow, back, table, prev_ref, before_ref,
        slot0, SB,
    )

    @pl.loop(0, pairs, unroll=unrolled(pairs))
    def _(q):
        high, low = split_pair(table, q, SB, padded)
        out[0, q, :, 0:HALF] = high
        out[0, q, :, HALF : 2 * HALF] = low


def ahead(tables, first, pairs, begin, blocks, prev, before):
    x, start_low, start_high, grow, back = tables
    padded = start_low.shape[0]
    full = [pl.BlockSpec(t.shape, lambda b: (0, 0)) for t in (prev, before) + tables]
    state = jax.ShapeDtypeStruct((padded, HALF), jnp.float32)
    return pl.pallas_call(
        functools.partial(ahead_kernel, begin),
        out_shape=(
            jax.ShapeDtypeStruct((blocks, pairs, SB, 2 * HALF), jnp.bfloat16),
            state,
            state,
        ),
        grid=(blocks,),
        in_specs=[pl.BlockSpec(memory_space=pltpu.SMEM)] + full,
        out_specs=(
            pl.BlockSpec((1, pairs, SB, 2 * HALF), lambda b: (b, 0, 0, 0)),
            pl.BlockSpec((padded, HALF), lambda b: (0, 0)),
            pl.BlockSpec((padded, HALF), lambda b: (0, 0)),
        ),
        scratch_shapes=[pltpu.VMEM((HALF // 128, SB * padded, 128), jnp.float32)],
        cost_estimate=pl.CostEstimate(
            flops=blocks * 6_000_000_000, bytes_accessed=blocks * 7_000_000, transcendentals=0
        ),
        name=f"ahead{begin}",
    )(first, prev, before, x, start_low, start_high, grow, back)


def legendre_kernel(
    width, first, raw, ready, later, prev_in, before_in, x_ref, start_low, start_high, grow, back, out,
    fields, table, prev_ref, before_ref,
):
    pairs = out.shape[0]
    padded = prev_ref.shape[0]
    first_pair = first[0]
    b = pl.program_id(0)
    slot0 = pl.multiple_of(b * SB, SB)

    def finish(q, high, low, count):
        dims = (((1,), (1,)), ((), ()))
        field = fields[q]
        sums = lax.dot_general(high, field, dims, preferred_element_type=jnp.float32)
        sums += lax.dot_general(low, field, dims, preferred_element_type=jnp.float32)
        sums = sums.T
        slots = lax.broadcasted_iota(jnp.int32, (2 * LEV, count), 1) + slot0
        length = M - first_pair - q
        is_low = slots < length
        odd = jnp.where(is_low, slots, slots + length) % 2
        sign = jnp.where(odd == 1, -1.0, 1.0)
        c = 2 * LEV
        north = jnp.where(is_low, sums[0:c], sums[2 * c : 3 * c])
        southern = jnp.where(is_low, sums[c : 2 * c], sums[3 * c : 4 * c])
        return (north + sign * southern) * (1.0 / SCALE)

    def step(count):
        recur(
            first_pair, x_ref[...], start_low, start_high, grow, back, table, prev_ref,
            before_ref, slot0, count,
        )

    @pl.when(b == 0)
    def _():
        prev_ref[...] = prev_in[...]
        before_ref[...] = before_in[...]

        @pl.loop(0, pairs, unroll=unrolled(pairs))
        def _(q):
            c = 2 * LEV
            for upper in range(2):
                part = raw[q, upper * c : (upper + 1) * c, :]
                bands = [
                    part[:, at : at + width] for at in range(NLAT - width, HALF - 1, -width)
                ]
                fields[q, 2 * upper * c : (2 * upper + 1) * c, :] = part[:, 0:HALF]
                fields[q, (2 * upper + 1) * c : (2 * upper + 2) * c, :] = jnp.concatenate(
                    bands, axis=1
                )

    def from_store(store):
        @pl.loop(0, pairs, unroll=unrolled(pairs))
        def _(q):
            high = store[0, q, :, 0:HALF]
            low = store[0, q, :, HALF : 2 * HALF]
            out[q, :, pl.ds(slot0, SB)] = finish(q, high, low, SB)

    @pl.when(b < EARLY)
    def _():
        from_store(ready)

    @pl.when((b >= EARLY) & (b < EARLY + LATER))
    def _():
        from_store(later)

    @pl.when((b >= EARLY + LATER) & (b < M // SB))
    def _():
        step(SB)

        @pl.loop(0, pairs, unroll=unrolled(pairs))
        def _(q):
            high, low = split_pair(table, q, SB, padded)
            out[q, :, pl.ds(slot0, SB)] = finish(q, high, low, SB)

    @pl.when(b == M // SB)
    def _():
        step(8)

        @pl.loop(0, pairs, unroll=unrolled(pairs))
        def _(q):
            high, low = split_pair(table, q, 8, padded)
            out[q, :, M : M + 1] = finish(q, high, low, 8)[:, 0:1]


def legendre(raw, tables, first, ready, late, width):
    x, start_low, start_high, grow, back = tables
    later, prev, before = late
    pairs = raw.shape[0]
    padded = start_low.shape[0]
    full = [pl.BlockSpec(t.shape, lambda b: (0, 0)) for t in (prev, before) + tables]
    return pl.pallas_call(
        functools.partial(legendre_kernel, width),
        out_shape=jax.ShapeDtypeStruct((pairs, 2 * LEV, M + 1), jnp.float32),
        grid=(M // SB + 1,),
        in_specs=[
            pl.BlockSpec(memory_space=pltpu.SMEM),
            pl.BlockSpec(raw.shape, lambda b: (0, 0, 0)),
            pl.BlockSpec(
                (1, pairs, SB, 2 * HALF), lambda b: (jnp.minimum(b, EARLY - 1), 0, 0, 0)
            ),
            pl.BlockSpec(
                (1, pairs, SB, 2 * HALF),
                lambda b: (jnp.clip(b - EARLY, 0, LATER - 1), 0, 0, 0),
            ),
        ]
        + full,
        out_specs=pl.BlockSpec((pairs, 2 * LEV, M + 1), lambda b: (0, 0, 0)),
        scratch_shapes=[
            pltpu.VMEM((pairs, 8 * LEV, HALF), jnp.bfloat16),
            pltpu.VMEM((HALF // 128, SB * padded, 128), jnp.float32),
            pltpu.VMEM((padded, HALF), jnp.float32),
            pltpu.VMEM((padded, HALF), jnp.float32),
        ],
        name="legendre",
    )(first, raw, ready, later, prev, before, x, start_low, start_high, grow, back)


def legendre_tables(first, pairs):
    padded = -(-pairs // 8) * 8
    pair_ids = first + jnp.arange(padded, dtype=jnp.int32)
    latitude = jnp.arange(HALF, dtype=jnp.int32).astype(jnp.float32)
    colat = math.pi * (latitude + 0.75) / (NLAT + 0.5)
    weights = math.pi * jnp.sin(colat) * math.sqrt(NLAT) / (NLAT + 0.5)
    cosine = jnp.cos(colat)
    log_sine = jnp.log(jnp.sin(colat))
    steps = jnp.arange(1, M, dtype=jnp.int32).astype(jnp.float32)
    terms = 0.5 * jnp.log1p(0.5 / steps)
    norm_logs = jnp.concatenate([jnp.zeros((1,), jnp.float32), jnp.cumsum(terms)])
    norm_logs = norm_logs + 0.5 * math.log(0.5)
    orders = jnp.arange(M, dtype=jnp.int32)
    high_order = M - 1 - pair_ids
    low_length = (M - pair_ids)[:, None]

    def sectoral(order):
        picked = jnp.sum(
            jnp.where(order[:, None] == orders[None, :], norm_logs[None, :], 0.0), axis=1
        )
        exponent = picked[:, None] + order.astype(jnp.float32)[:, None] * log_sine[None, :]
        ramp = jnp.clip((exponent + 75.0) / 10.0, 0.0, 1.0)
        value = jnp.exp(jnp.maximum(exponent, -75.0)) * ramp
        return value * (weights * SCALE)[None, :]

    slot = jnp.arange(M + SB, dtype=jnp.int32)[None, :]
    is_low = slot < low_length
    order = jnp.where(is_low, pair_ids[:, None], high_order[:, None])
    degree = order + jnp.where(is_low, slot, slot - low_length)
    order_f = order.astype(jnp.float32)
    degree_f = degree.astype(jnp.float32)
    lower_f = degree_f - 1.0
    grows = degree > order
    ratio = jnp.where(
        grows,
        (4.0 * degree_f * degree_f - 1.0)
        / jnp.where(grows, degree_f * degree_f - order_f * order_f, 1.0),
        0.0,
    )
    behind = degree - 1 > order
    inverse = jnp.where(
        behind,
        (lower_f * lower_f - order_f * order_f)
        / jnp.where(behind, 4.0 * lower_f * lower_f - 1.0, 1.0),
        0.0,
    )
    grow = jnp.sqrt(ratio)
    back = grow * jnp.sqrt(inverse)
    return cosine[None, :], sectoral(pair_ids), sectoral(high_order), grow, back


def body(source, row_map, col_map, pattern, codes, need_list, owner):
    lat_count = lax.axis_size("lat")
    tile_count = lax.axis_size("tile")
    lat_me = lax.axis_index("lat")
    tile_me = lax.axis_index("tile")
    slots_dev = source.shape[0]
    block_ids = jnp.arange(owner.shape[0], dtype=jnp.int32)
    needs_column = need_list[0]
    holder = jnp.sum(
        jnp.where(needs_column[:, :, None] == block_ids[None, None, :], owner[None, None, :], 0),
        axis=2,
    )
    holder_lat = holder // slots_dev % lat_count
    holder_slot = holder % slots_dev
    my_lat = lax.dynamic_index_in_dim(holder_lat, lat_me, 0, keepdims=False)
    held_here = holder_lat == lat_me
    rank = jnp.cumsum(held_here.astype(jnp.int32), axis=1) - 1
    places = jnp.arange(MOST, dtype=jnp.int32)
    hit = held_here[:, None, :] & (rank[:, None, :] == places[None, :, None])
    picks = jnp.sum(jnp.where(hit, holder_slot[:, None, :], 0), axis=2)
    outgoing = jnp.take(source, picks.reshape(-1), axis=0).reshape(
        (lat_count, MOST) + source.shape[1:]
    )
    incoming = lax.all_to_all(outgoing, "lat", split_axis=0, concat_axis=0, tiled=True)
    earlier = jnp.arange(NEED)[:, None] > jnp.arange(NEED)[None, :]
    same = (my_lat[:, None] == my_lat[None, :]) & earlier
    my_rank = jnp.sum(same.astype(jnp.int32), axis=1)
    place = my_lat * MOST + my_rank
    flat = incoming.reshape(lat_count * MOST, LEV, BS, BS)
    return place, flat


def whole(source, row_map, col_map, pattern, codes, need_list, owner):
    lat_count = lax.axis_size("lat")
    tile_count = lax.axis_size("tile")
    lat_me = lax.axis_index("lat")
    tile_me = lax.axis_index("tile")
    place, flat = body(source, row_map, col_map, pattern, codes, need_list, owner)
    held = flat.shape[0]
    uses = pattern[:, 0].reshape(-1)
    wanted = jnp.arange(NEED, dtype=jnp.int32)
    pos = jnp.sum(jnp.where(uses[:, None] == wanted[None, :], place[None, :], 0), axis=1)
    code = codes[:, 0].reshape(-1)
    blocks = flat.reshape(held, LEV * BS, BS)
    turned = jnp.swapaxes(flat, 2, 3).reshape(held, LEV * BS, BS)
    south = (lat_me >= lat_count // 2).astype(jnp.int32).reshape(1)
    field = regrid(blocks, turned, row_map, col_map, pos, code, south)

    pairs = M // 2 // (tile_count * lat_count)
    first = (tile_me * lat_count + lat_me) * pairs
    tables = legendre_tables(first, pairs)
    field, x = lax.optimization_barrier((field, tables[0]))
    tables = (x,) + tables[1:]
    zeros = jnp.zeros_like(tables[1])
    ready, prev, before = ahead(tables, first.reshape(1), pairs, 0, EARLY, zeros, zeros)

    flat_rows = field.reshape(LEV * field.shape[1], field.shape[2])
    rows = lax.all_to_all(flat_rows, "tile", split_axis=0, concat_axis=1, tiled=True)
    spectral = dft(rows, dft_tables())
    spectral, prev = lax.optimization_barrier((spectral, prev))
    late = ahead(tables, first.reshape(1), pairs, EARLY, LATER, prev, before)
    arranged = lax.all_to_all(spectral, ("tile", "lat"), split_axis=1, concat_axis=0, tiled=True)

    parts = tile_count // LEV
    count = rows.shape[0]
    box = arranged.reshape(LEV, parts, lat_count, 2, 2, pairs, count)
    raw = jnp.transpose(box, (5, 3, 4, 0, 2, 1, 6)).reshape(pairs, 4 * LEV, NLAT)
    return legendre(raw, tables, first.reshape(1), ready, late, NLAT // lat_count)


def solution(mesh):
    placed = (
        P(("tile", "lat"), None, None),
        P("lat", "tile", None, None, None),
        P("lat", None, None, "tile"),
        P("lat", "tile", None),
        P("lat", "tile", None),
        P("tile", None, None),
        P(),
    )
    return jax.shard_map(
        whole, mesh=mesh, in_specs=placed, out_specs=P(("tile", "lat"), None, None), check_vma=False
    )
```
